32 devices in a mesh: pair: 8 (over y, x, core), row: 4 (over z).
Axes of the slice: x: 2, y: 2, z: 4, core: 2. Of those that a mesh axis runs over, the one named last changes fastest.
Arguments:
- amplitudes: bfloat16 [3, 160, 32, 5120], P(None, 'pair', 'row'), may hold values from -6 to 6
- integrals: bfloat16 [3, 5120, 5120], P(None, 'row', 'pair'), may hold values from -0.078125 to 0.078125
- occupied_irrep: int32 [32], replicated, may hold values from 0 to 7
- virtual_order: int32 [1280], replicated, may hold values from 0 to 1279, each once
- block_irreps: int32 [3], replicated, may hold values from 0 to 7
- occupied_energy: float32 [32], replicated, may hold values from -2 to -0.5
- virtual_energy: float32 [1280], replicated, may hold values from 1 to 4
Outputs:
- update: float32 [3, 160, 32, 5120], P(None, None, 'row', 'pair')
The draws below stay inside these ranges and needn't reach their ends.
Inputs may be any that keep to these rules, and one draw needn't show every extreme that they name: virtual_order holds every virtual orbital once; entries g * 160 to g * 160 + 159 are the virtual orbitals of irrep g.
All inputs are finite; a program needn't handle non-finite values.
Results may differ from the reference program's by a relative error of at most 0.0003.
Values may be sent and summed in bfloat16 or wider, within the bound.
A program may use at most 128 MiB of HBM per device.

```python
import jax
import jax.numpy as jnp

NO = 32
VIRG = 160
IRREPS = 8
IRR = 3
NV = 1280
P_SIZE = 5120


def touch_ends(values, own_key, smallest, high):
    place = [jax.random.randint(jax.random.fold_in(own_key, axis), (), 0, length) for axis, length in enumerate(values.shape)]
    longest = values.shape.index(max(values.shape))
    neighbour = place[:longest] + [(place[longest] + 1) % values.shape[longest]] + place[longest + 1:]
    return values.at[tuple(place)].set(smallest).at[tuple(neighbour)].set(high)


def block_scale(rng, shape, pieces, low, high):
    gain = 1.0
    for dim, parts in pieces:
        draws = jax.random.uniform(jax.random.fold_in(jax.random.fold_in(rng, 6), dim), (parts,), jnp.float32, low / len(pieces), high / len(pieces))
        gain = gain * jnp.repeat(jnp.exp(draws), shape[dim] // parts).reshape((-1,) + (1,) * (len(shape) - 1 - dim))
    return gain


def scatter_about(own_key, dims, spread, reach, shards=(), kind=jnp.bfloat16):
    entries = spread * jax.random.normal(own_key, dims, jnp.float32)
    if shards:
        entries = entries * block_scale(own_key, dims, shards, -0.22, 0.18)
    return jnp.clip(entries, -reach, reach).astype(kind)


def setup_inputs(seed: int = 0) -> dict:
    splits = jax.random.split(jax.random.key(seed), 8)
    amplitudes = scatter_about(splits[0], (IRR, VIRG, NO, P_SIZE), 1.0, 6.0, ((1, 8), (2, 4)))
    integrals = scatter_about(splits[1], (IRR, P_SIZE, P_SIZE), P_SIZE ** -0.5, 0.078125, ((1, 4), (2, 8)))
    occupied_irrep = touch_ends(jax.random.randint(splits[2], (NO,), 0, IRREPS), jax.random.fold_in(splits[2], 1), 0, IRREPS - 1).astype(jnp.int32)
    virtual_order = jax.random.permutation(splits[3], NV).astype(jnp.int32)
    block_irreps = jax.random.randint(splits[4], (IRR,), 0, IRREPS).astype(jnp.int32)
    occupied_energy = jnp.clip(jax.random.uniform(splits[5], (NO,), jnp.float32, -2.0, -0.5), -2.0, -0.5)
    virtual_energy = jnp.clip(jax.random.uniform(splits[6], (NV,), jnp.float32, 1.0, 4.0), 1.0, 4.0)
    return {"amplitudes": amplitudes, "integrals": integrals, "occupied_irrep": occupied_irrep, "virtual_order": virtual_order, "block_irreps": block_irreps, "occupied_energy": occupied_energy, "virtual_energy": virtual_energy}


def shift_table(occupied_irrep, virtual_order, block_irreps, occupied_energy, virtual_energy):
    pair_irrep = jnp.bitwise_xor(block_irreps[:, None], occupied_irrep[None, :]).astype(jnp.int32)
    orbital_slot = pair_irrep[:, None, :] * VIRG + jnp.arange(VIRG, dtype=jnp.int32)[None, :, None]
    orbital_index = jnp.take(virtual_order, orbital_slot.astype(jnp.int32))
    return jnp.take(virtual_energy, orbital_index) - occupied_energy[None, None, :]


def reference(amplitudes, integrals, occupied_irrep, virtual_order, block_irreps, occupied_energy, virtual_energy):
    shift = shift_table(occupied_irrep, virtual_order, block_irreps, occupied_energy, virtual_energy)
    results = []
    for irrep_block in range(IRR):
        matrix = amplitudes[irrep_block].reshape(VIRG * NO, P_SIZE)
        cycle_term = jnp.dot(matrix, integrals[irrep_block], preferred_element_type=jnp.float32)
        flat_shift = shift[irrep_block].reshape(VIRG * NO)
        denominator = flat_shift[:, None] + flat_shift[None, :]
        results.append((cycle_term / denominator).reshape(VIRG, NO, P_SIZE))
    return jnp.stack(results)
```

```python
import jax
import jax.numpy as jnp
from jax import lax
from jax.sharding import PartitionSpec as P

VIRG = 160


def shift_table(occupied_irrep, virtual_order, block_irreps, occupied_energy, virtual_energy):
    count_virt = virtual_energy.shape[0]
    orbital_ids = jnp.arange(count_virt, dtype=jnp.int32)
    matches = virtual_order[:, None] == orbital_ids[None, :]
    slot_energy = jnp.sum(jnp.where(matches, virtual_energy[None, :], jnp.float32(0.0)), axis=1)
    irrep_count = count_virt // VIRG
    energy_grid = slot_energy.reshape(irrep_count, VIRG)
    pair_irrep = jnp.bitwise_xor(block_irreps[:, None], occupied_irrep[None, :])
    irrep_ids = jnp.arange(irrep_count, dtype=jnp.int32)
    chosen = pair_irrep[:, None, None, :] == irrep_ids[None, :, None, None]
    picked = jnp.sum(jnp.where(chosen, energy_grid[None, :, :, None], jnp.float32(0.0)), axis=1)
    return picked - occupied_energy[None, None, :]


def body(
    amplitudes,
    integrals,
    occupied_irrep,
    virtual_order,
    block_irreps,
    occupied_energy,
    virtual_energy,
):
    block_count, virt_local, occ_local, pair_width = amplitudes.shape
    column_width = integrals.shape[2]
    shift = shift_table(
        occupied_irrep, virtual_order, block_irreps, occupied_energy, virtual_energy
    )
    occ_start = lax.axis_index("row") * occ_local
    col_start = lax.axis_index("pair") * column_width
    results = []
    for block in range(block_count):
        whole_rows = lax.all_gather(integrals[block], "row", axis=0, tiled=True)
        piece = lax.all_gather(amplitudes[block], "pair", axis=0, tiled=True)
        flat = piece.reshape(piece.shape[0] * piece.shape[1], piece.shape[2])
        product = jnp.dot(flat, whole_rows, preferred_element_type=jnp.float32)
        cycle_term = product.reshape(piece.shape[0], piece.shape[1], whole_rows.shape[1])
        row_shift = lax.dynamic_slice_in_dim(shift[block], occ_start, occ_local, 1)
        col_shift = lax.dynamic_slice_in_dim(
            shift[block].reshape(pair_width), col_start, column_width, 0
        )
        denominator = row_shift[:, :, None] + col_shift[None, None, :]
        results.append(cycle_term / denominator)
    return jnp.stack(results)


def gather_integrals(mine):
    row = lax.axis_index("row")
    near = lax.ppermute(mine, "row", [(0, 1), (1, 0), (2, 3), (3, 2)])
    far_inner = lax.ppermute(mine, "row", [(1, 2), (2, 1)])
    far_outer = lax.ppermute(near, "row", [(1, 2), (2, 1)])
    end_inner = lax.ppermute(far_inner, "row", [(1, 0), (2, 3)])
    end_outer = lax.ppermute(far_outer, "row", [(1, 0), (2, 3)])
    inner = jnp.where((row == 1) | (row == 2), far_inner, end_inner)
    outer = jnp.where((row == 1) | (row == 2), far_outer, end_outer)
    even = row % 2 == 0
    first = jnp.where(even, mine, near)
    second = jnp.where(even, near, mine)
    low = row < 2
    return jnp.concatenate(
        [
            jnp.where(low, first, outer),
            jnp.where(low, second, inner),
            jnp.where(low, inner, first),
            jnp.where(low, outer, second),
        ]
    )


def gather_amplitudes(mine):
    pair = lax.axis_index("pair")
    spot = pair // 2
    whole = jnp.zeros((4,) + mine.shape, mine.dtype)
    whole = lax.dynamic_update_slice_in_dim(whole, mine[None], spot, 0)
    for step in (1, 2, 3):
        came = lax.ppermute(mine, "pair", [(p, p ^ (2 * step)) for p in range(8)])
        whole = lax.dynamic_update_slice_in_dim(whole, came[None], spot ^ step, 0)
    other = lax.ppermute(whole, "pair", [(p, p ^ 1) for p in range(8)])
    return whole, other


def linked_body(
    amplitudes,
    integrals,
    occupied_irrep,
    virtual_order,
    block_irreps,
    occupied_energy,
    virtual_energy,
):
    block_count, virt_local, occ_local, pair_width = amplitudes.shape
    column_width = integrals.shape[2]
    shift = shift_table(
        occupied_irrep, virtual_order, block_irreps, occupied_energy, virtual_energy
    )
    occ_start = lax.axis_index("row") * occ_local
    pair = lax.axis_index("pair")
    core = pair % 2
    results = []
    for block in range(block_count):
        whole_rows = gather_integrals(integrals[block])
        pieces = gather_amplitudes(amplitudes[block])
        row_shift = lax.dynamic_slice_in_dim(shift[block], occ_start, occ_local, 1)
        row_shift = row_shift.reshape(4, 2, virt_local, occ_local)
        col_shift = lax.dynamic_slice_in_dim(
            shift[block].reshape(pair_width), pair * column_width, column_width, 0
        )
        halves = []
        for side, piece in enumerate(pieces):
            product = jnp.dot(
                piece.reshape(-1, pair_width), whole_rows, preferred_element_type=jnp.float32
            ).reshape(4, virt_local, occ_local, column_width)
            part_shift = lax.dynamic_index_in_dim(row_shift, core ^ side, 1, keepdims=False)
            halves.append(product / (part_shift[..., None] + col_shift))
        even = core == 0
        both = jnp.stack(
            [jnp.where(even, halves[0], halves[1]), jnp.where(even, halves[1], halves[0])], 1
        )
        results.append(both.reshape(8 * virt_local, occ_local, column_width))
    return jnp.stack(results)


def solution(mesh):
    placed = (P(None, "pair", "row", None), P(None, "row", "pair"), P(), P(), P(), P(), P())
    linked = mesh.shape["pair"] == 8 and mesh.shape["row"] == 4
    return jax.shard_map(
        linked_body if linked else body,
        mesh=mesh,
        in_specs=placed,
        out_specs=P(None, None, "row", "pair"),
        check_vma=False,
    )
```

```python
import jax
import jax.numpy as jnp
from jax import lax
from jax.experimental import pallas as pl
from jax.experimental.pallas import tpu as pltpu
from jax.sharding import PartitionSpec as P

VIRG = 160


def shift_table(occupied_irrep, virtual_order, block_irreps, occupied_energy, virtual_energy):
    count_virt = virtual_energy.shape[0]
    orbital_ids = jnp.arange(count_virt, dtype=jnp.int32)
    matches = virtual_order[:, None] == orbital_ids[None, :]
    slot_energy = jnp.sum(jnp.where(matches, virtual_energy[None, :], jnp.float32(0.0)), axis=1)
    irrep_count = count_virt // VIRG
    energy_grid = slot_energy.reshape(irrep_count, VIRG)
    pair_irrep = jnp.bitwise_xor(block_irreps[:, None], occupied_irrep[None, :])
    irrep_ids = jnp.arange(irrep_count, dtype=jnp.int32)
    chosen = pair_irrep[:, None, None, :] == irrep_ids[None, :, None, None]
    picked = jnp.sum(jnp.where(chosen, energy_grid[None, :, :, None], jnp.float32(0.0)), axis=1)
    return picked - occupied_energy[None, None, :]


def body(
    amplitudes,
    integrals,
    occupied_irrep,
    virtual_order,
    block_irreps,
    occupied_energy,
    virtual_energy,
):
    block_count, virt_local, occ_local, pair_width = amplitudes.shape
    column_width = integrals.shape[2]
    shift = shift_table(
        occupied_irrep, virtual_order, block_irreps, occupied_energy, virtual_energy
    )
    occ_start = lax.axis_index("row") * occ_local
    col_start = lax.axis_index("pair") * column_width
    results = []
    for block in range(block_count):
        whole_rows = lax.all_gather(integrals[block], "row", axis=0, tiled=True)
        piece = lax.all_gather(amplitudes[block], "pair", axis=0, tiled=True)
        flat = piece.reshape(piece.shape[0] * piece.shape[1], piece.shape[2])
        product = jnp.dot(flat, whole_rows, preferred_element_type=jnp.float32)
        cycle_term = product.reshape(piece.shape[0], piece.shape[1], whole_rows.shape[1])
        row_shift = lax.dynamic_slice_in_dim(shift[block], occ_start, occ_local, 1)
        col_shift = lax.dynamic_slice_in_dim(
            shift[block].reshape(pair_width), col_start, column_width, 0
        )
        denominator = row_shift[:, :, None] + col_shift[None, None, :]
        results.append(cycle_term / denominator)
    return jnp.stack(results)


def kernel(a_ref, b_ref, cycle_ref, all_a, all_b, z_send, z_recv, p_send, p_recv, own_sem):
    blocks = a_ref.shape[0]
    pair = lax.axis_index("pair")
    row = lax.axis_index("row")
    near = row ^ 1
    across = 3 - row
    is_inner = (row == 1) | (row == 2)

    barrier = pltpu.get_barrier_semaphore()
    friends = [(pair, near), (pair, across)] + [(pair ^ step, row) for step in (1, 2, 4, 6)]
    for friend in friends:
        pl.semaphore_signal(
            barrier, inc=1, device_id=friend, device_id_type=pl.DeviceIdType.MESH
        )
    pl.semaphore_wait(barrier, len(friends))

    def z_copy(kind, block):
        source, slot, target = {
            "near": (b_ref.at[block], row, near),
            "mid_own": (b_ref.at[block], row, across),
            "mid_near": (all_b.at[block, near], near, across),
            "end_inner": (all_b.at[block, across], across, near),
            "end_outer": (all_b.at[block, across ^ 1], across ^ 1, near),
        }[kind]
        place = ["near", "mid_own", "mid_near", "end_inner", "end_outer"].index(kind)
        return pltpu.make_async_remote_copy(
            src_ref=source,
            dst_ref=all_b.at[block, slot],
            send_sem=z_send.at[place, block],
            recv_sem=z_recv.at[place, block],
            device_id=(pair, target),
            device_id_type=pl.DeviceIdType.MESH,
        )

    def plane_copy(step, block):
        return pltpu.make_async_remote_copy(
            src_ref=a_ref.at[block],
            dst_ref=all_a.at[block, pair],
            send_sem=p_send.at[step - 1, block],
            recv_sem=p_recv.at[step - 1, block],
            device_id=(pair ^ (2 * step), row),
            device_id_type=pl.DeviceIdType.MESH,
        )

    def core_copy(step, block):
        piece = pair ^ (2 * step)
        return pltpu.make_async_remote_copy(
            src_ref=a_ref.at[block] if step == 0 else all_a.at[block, piece],
            dst_ref=all_a.at[block, piece],
            send_sem=p_send.at[3 + step, block],
            recv_sem=p_recv.at[3 + step, block],
            device_id=(pair ^ 1, row),
            device_id_type=pl.DeviceIdType.MESH,
        )

    def own_copies(block):
        return [
            pltpu.make_async_copy(a_ref.at[block], all_a.at[block, pair], own_sem.at[0, block]),
            pltpu.make_async_copy(b_ref.at[block], all_b.at[block, row], own_sem.at[1, block]),
        ]

    def plane_start(block):
        for step in (1, 2, 3):
            plane_copy(step, block).start()
        core_copy(0, block).start()

    def plane_forward(block):
        for step in (1, 2, 3):
            plane_copy(step, block).wait_recv()
            core_copy(step, block).start()

    def multiply(block):
        for copy in own_copies(block):
            copy.wait()
        for step in range(4):
            core_copy(step, block).wait_recv()

        @pl.when(jnp.logical_not(is_inner))
        def _():
            z_copy("end_inner", block).wait_recv()
            z_copy("end_outer", block).wait_recv()

        def tile(a_tile, b_tile, c_tile):
            rows = a_tile.shape[0] * a_tile.shape[1]
            depth = b_tile.shape[1]

            def add(part, total):
                start = pl.multiple_of(part * depth, depth)
                left = a_tile[:, :, pl.ds(start, depth)].reshape(rows, depth)
                return total + jnp.dot(left, b_tile[part], preferred_element_type=jnp.float32)

            c_tile[...] = lax.fori_loop(
                0, b_tile.shape[0], add, jnp.zeros(c_tile.shape, jnp.float32)
            )

        count, rows, width = all_a.shape[1:]
        pltpu.emit_pipeline(
            tile,
            grid=(count // 2,),
            in_specs=[
                pl.BlockSpec((2, rows, width), lambda i: (i, 0, 0)),
                pl.BlockSpec(all_b.shape[1:], lambda i: (0, 0, 0)),
            ],
            out_specs=[pl.BlockSpec((2 * rows, cycle_ref.shape[2]), lambda i: (i, 0))],
        )(all_a.at[block], all_b.at[block], cycle_ref.at[block])

    z_copy("near", 0).start()
    plane_start(0)

    @pl.when(is_inner)
    def _():
        z_copy("mid_own", 0).start()

    plane_start(1)
    for block in range(blocks):
        for copy in own_copies(block):
            copy.start()
    for block in range(blocks):
        z_copy("near", block).wait_recv()
        if block + 1 < blocks:
            z_copy("near", block + 1).start()

        @pl.when(is_inner)
        def _():
            z_copy("mid_near", block).start()
            z_copy("mid_own", block).wait_recv()
            z_copy("end_inner", block).start()
            if block + 1 < blocks:
                z_copy("mid_own", block + 1).start()
            z_copy("mid_near", block).wait_recv()
            z_copy("end_outer", block).start()

        plane_forward(block)
        if block + 2 < blocks:
            plane_start(block + 2)
        if block >= 1 and block + 1 < blocks:
            multiply(block - 1)
    for block in range(max(blocks - 2, 0), blocks):
        multiply(block)
    for block in range(blocks):
        z_copy("near", block).wait_send()
        for step in (1, 2, 3):
            plane_copy(step, block).wait_send()
        for step in range(4):
            core_copy(step, block).wait_send()

        @pl.when(is_inner)
        def _():
            for kind in ("mid_own", "mid_near", "end_inner", "end_outer"):
                z_copy(kind, block).wait_send()


def linked_body(
    amplitudes,
    integrals,
    occupied_irrep,
    virtual_order,
    block_irreps,
    occupied_energy,
    virtual_energy,
):
    blocks, virt_local, occ_local, pair_width = amplitudes.shape
    depth, column_width = integrals.shape[1:]
    rows = virt_local * occ_local
    shift = shift_table(
        occupied_irrep, virtual_order, block_irreps, occupied_energy, virtual_energy
    )
    row_shift = lax.dynamic_slice_in_dim(shift, lax.axis_index("row") * occ_local, occ_local, 2)
    col_shift = lax.dynamic_slice_in_dim(
        shift.reshape(blocks, pair_width), lax.axis_index("pair") * column_width, column_width, 1
    )
    cycle_term = pl.pallas_call(
        kernel,
        out_shape=(
            jax.ShapeDtypeStruct((blocks, 8 * rows, column_width), jnp.float32),
            jax.ShapeDtypeStruct((blocks, 8, rows, pair_width), jnp.bfloat16),
            jax.ShapeDtypeStruct((blocks, 4, depth, column_width), jnp.bfloat16),
        ),
        in_specs=[pl.BlockSpec(memory_space=pl.ANY)] * 2,
        out_specs=(pl.BlockSpec(memory_space=pl.ANY),) * 3,
        scratch_shapes=[
            pltpu.SemaphoreType.DMA((5, blocks)),
            pltpu.SemaphoreType.DMA((5, blocks)),
            pltpu.SemaphoreType.DMA((7, blocks)),
            pltpu.SemaphoreType.DMA((7, blocks)),
            pltpu.SemaphoreType.DMA((2, blocks)),
        ],
        compiler_params=pltpu.CompilerParams(
            collective_id=0, has_side_effects=True, vmem_limit_bytes=50 * 2**20
        ),
    )(amplitudes.reshape(blocks, rows, pair_width), integrals)[0]
    cycle_term = cycle_term.reshape(blocks, 8 * virt_local, occ_local, column_width)
    return cycle_term / (row_shift[..., None] + col_shift[:, None, None, :])


def solution(mesh):
    placed = (P(None, "pair", "row", None), P(None, "row", "pair"), P(), P(), P(), P(), P())
    linked = mesh.shape["pair"] == 8 and mesh.shape["row"] == 4
    return jax.shard_map(
        linked_body if linked else body,
        mesh=mesh,
        in_specs=placed,
        out_specs=P(None, None, "row", "pair"),
        check_vma=False,
    )
```

```python
import jax
import jax.numpy as jnp
from jax import lax
from jax.experimental import pallas as pl
from jax.experimental.pallas import tpu as pltpu
from jax.sharding import PartitionSpec as P

VIRG = 160


def shift_table(occupied_irrep, virtual_order, block_irreps, occupied_energy, virtual_energy):
    count_virt = virtual_energy.shape[0]
    orbital_ids = jnp.arange(count_virt, dtype=jnp.int32)
    matches = virtual_order[:, None] == orbital_ids[None, :]
    slot_energy = jnp.sum(jnp.where(matches, virtual_energy[None, :], jnp.float32(0.0)), axis=1)
    irrep_count = count_virt // VIRG
    energy_grid = slot_energy.reshape(irrep_count, VIRG)
    pair_irrep = jnp.bitwise_xor(block_irreps[:, None], occupied_irrep[None, :])
    irrep_ids = jnp.arange(irrep_count, dtype=jnp.int32)
    chosen = pair_irrep[:, None, None, :] == irrep_ids[None, :, None, None]
    picked = jnp.sum(jnp.where(chosen, energy_grid[None, :, :, None], jnp.float32(0.0)), axis=1)
    return picked - occupied_energy[None, None, :]


def body(
    amplitudes,
    integrals,
    occupied_irrep,
    virtual_order,
    block_irreps,
    occupied_energy,
    virtual_energy,
):
    block_count, virt_local, occ_local, pair_width = amplitudes.shape
    column_width = integrals.shape[2]
    shift = shift_table(
        occupied_irrep, virtual_order, block_irreps, occupied_energy, virtual_energy
    )
    occ_start = lax.axis_index("row") * occ_local
    col_start = lax.axis_index("pair") * column_width
    results = []
    for block in range(block_count):
        whole_rows = lax.all_gather(integrals[block], "row", axis=0, tiled=True)
        piece = lax.all_gather(amplitudes[block], "pair", axis=0, tiled=True)
        flat = piece.reshape(piece.shape[0] * piece.shape[1], piece.shape[2])
        product = jnp.dot(flat, whole_rows, preferred_element_type=jnp.float32)
        cycle_term = product.reshape(piece.shape[0], piece.shape[1], whole_rows.shape[1])
        row_shift = lax.dynamic_slice_in_dim(shift[block], occ_start, occ_local, 1)
        col_shift = lax.dynamic_slice_in_dim(
            shift[block].reshape(pair_width), col_start, column_width, 0
        )
        denominator = row_shift[:, :, None] + col_shift[None, None, :]
        results.append(cycle_term / denominator)
    return jnp.stack(results)


HELPED = (1, 2)
PIECES = ((0, 256), (256, 384))


def kernel(
    a_ref, b_ref, cycle_ref, all_a, all_b, end_a, part_out, part_in,
    z_send, z_recv, p_send, p_recv, own_sem,
):
    blocks, rows, width = a_ref.shape
    depth = b_ref.shape[1]
    half = rows // 2
    pair = lax.axis_index("pair")
    row = lax.axis_index("row")
    near = row ^ 1
    across = 3 - row
    is_inner = (row == 1) | (row == 2)
    is_outer = jnp.logical_not(is_inner)

    barrier = pltpu.get_barrier_semaphore()
    friends = [(pair, near), (pair, across)] + [(pair ^ step, row) for step in (1, 2, 4)]
    for friend in friends:
        pl.semaphore_signal(
            barrier, inc=1, device_id=friend, device_id_type=pl.DeviceIdType.MESH
        )
    pl.semaphore_wait(barrier, len(friends))

    kinds = ["near", "mid_own", "mid_near", "end_inner", "end_outer", "end_a", "part"]

    def z_copy(kind, block, piece=None):
        place = 2 * kinds.index(kind) + (piece or 0)
        cols = pl.ds(*PIECES[piece]) if piece is not None else slice(None)
        if kind == "near":
            source, dest, target = b_ref.at[block], all_b.at[block, row], near
        elif kind == "mid_own":
            source, dest = b_ref.at[block, :, cols], all_b.at[block, row, :, cols]
            target = across
        elif kind == "mid_near":
            source = dest = all_b.at[block, near, :, cols]
            target = across
        elif kind == "end_inner":
            source = dest = all_b.at[block, across]
            target = near
        elif kind == "end_outer":
            source = dest = all_b.at[block, across ^ 1]
            target = near
        elif kind == "end_a":
            start = pl.multiple_of(((3 - row) // 3) * depth, depth)
            source = a_ref.at[block, :, pl.ds(start, width - depth)]
            dest = end_a.at[HELPED.index(block), pair]
            target = near
        else:
            source = part_out.at[HELPED.index(block), :, cols]
            dest = part_in.at[HELPED.index(block), :, cols]
            target = near
        return pltpu.make_async_remote_copy(
            src_ref=source,
            dst_ref=dest,
            send_sem=z_send.at[place, block],
            recv_sem=z_recv.at[place, block],
            device_id=(pair, target),
            device_id_type=pl.DeviceIdType.MESH,
        )

    class Gather:
        def __init__(self, number, own, whole):
            self.number, self.own, self.whole = number, own, whole

        def copy(self, kind):
            whole = self.whole
            top, bottom = pl.ds(0, half), pl.ds(half, half)
            source, dest, step = [
                (self.own, whole.at[pair], 2),
                (self.own, whole.at[pair], 4),
                (whole.at[pair ^ 4, bottom], whole.at[pair ^ 4, bottom], 2),
                (whole.at[pair ^ 2, top], whole.at[pair ^ 2, top], 4),
                (self.own, whole.at[pair], 1),
                (whole.at[pair ^ 2], whole.at[pair ^ 2], 1),
                (whole.at[pair ^ 4], whole.at[pair ^ 4], 1),
                (whole.at[pair ^ 6], whole.at[pair ^ 6], 1),
            ][kind]
            return pltpu.make_async_remote_copy(
                src_ref=source,
                dst_ref=dest,
                send_sem=p_send.at[kind, self.number],
                recv_sem=p_recv.at[kind, self.number],
                device_id=(pair ^ step, row),
                device_id_type=pl.DeviceIdType.MESH,
            )

        def first(self):
            for kind in (0, 1, 4):
                self.copy(kind).start()

        def second(self):
            self.copy(0).wait_recv()
            self.copy(3).start()
            self.copy(5).start()
            self.copy(1).wait_recv()
            self.copy(2).start()
            self.copy(6).start()

        def third(self):
            self.copy(2).wait_recv()
            self.copy(3).wait_recv()
            self.copy(7).start()

        def finish(self):
            for kind in (4, 5, 6, 7):
                self.copy(kind).wait_recv()

        def drain(self):
            for kind in range(8):
                self.copy(kind).wait_send()

    plane = [Gather(block, a_ref.at[block], all_a.at[block]) for block in range(blocks)]
    ends = [
        Gather(blocks + spot, end_a.at[spot, pair], end_a.at[spot]) for spot in range(len(HELPED))
    ]

    def own_copies(block):
        return [
            pltpu.make_async_copy(a_ref.at[block], all_a.at[block, pair], own_sem.at[0, block]),
            pltpu.make_async_copy(b_ref.at[block], all_b.at[block, row], own_sem.at[1, block]),
        ]

    def chain(a_tile, b_tile, low, high, total):
        def add(part, total):
            start = pl.multiple_of(part * depth, depth)
            left = a_tile[:, :, pl.ds(start, depth)].reshape(-1, depth)
            return total + jnp.dot(left, b_tile[part], preferred_element_type=jnp.float32)

        return lax.fori_loop(low, high, add, total)

    def help_end(block, piece):
        spot = HELPED.index(block)
        z_copy("mid_own", block, piece).wait_recv()
        z_copy("mid_near", block, piece).wait_recv()
        if piece == 0:
            own_copies(block)[1].wait()
        cols = pl.ds(*PIECES[piece])
        size = PIECES[piece][1]

        def tile(a_tile, b_tile, c_tile):
            c_tile[...] = chain(
                a_tile, b_tile, 0, b_tile.shape[0], jnp.zeros(c_tile.shape, jnp.float32)
            )

        pltpu.emit_pipeline(
            tile,
            grid=(4,),
            in_specs=[
                pl.BlockSpec((2, rows, width - depth), lambda i: (i, 0, 0)),
                pl.BlockSpec((3, depth, size), lambda i: (0, 0, 0)),
            ],
            out_specs=[pl.BlockSpec((2 * rows, size), lambda i: (i, 0))],
        )(
            end_a.at[spot],
            all_b.at[block, pl.ds(2 - row, 3), :, cols],
            part_out.at[spot, :, cols],
        )
        z_copy("part", block, piece).start()

    def multiply(block):
        helped = block in HELPED
        own_copies(block)[0].wait()
        plane[block].finish()

        @pl.when(is_outer)
        def _():
            own_copies(block)[1].wait()
            if helped:
                for piece in range(len(PIECES)):
                    z_copy("part", block, piece).wait_recv()
            else:
                z_copy("end_inner", block).wait_recv()
                z_copy("end_outer", block).wait_recv()

        if not helped:

            @pl.when(is_inner)
            def _():
                own_copies(block)[1].wait()

        low = jnp.where(is_inner, 0, row) if helped else 0
        high = jnp.where(is_inner, 4, row + 1) if helped else 4

        def tile(a_tile, b_tile, *rest):
            c_tile = rest[-1]
            total = jnp.zeros(c_tile.shape, jnp.float32)
            if helped:
                total = jnp.where(is_outer, rest[0][...], total)
            c_tile[...] = chain(a_tile, b_tile, low, high, total)

        square = pl.BlockSpec((2 * rows, cycle_ref.shape[2]), lambda i: (i, 0))
        extra = [part_in.at[HELPED.index(block)]] if helped else []
        pltpu.emit_pipeline(
            tile,
            grid=(4,),
            in_specs=[
                pl.BlockSpec((2, rows, width), lambda i: (i, 0, 0)),
                pl.BlockSpec(all_b.shape[1:], lambda i: (0, 0, 0)),
            ]
            + [square] * len(extra),
            out_specs=[square],
        )(all_a.at[block], all_b.at[block], *extra, cycle_ref.at[block])

    both = range(len(PIECES))
    z_copy("near", 0).start()
    plane[0].first()

    @pl.when(is_inner)
    def _():
        z_copy("mid_own", 0).start()

    for block in range(blocks):
        for copy in own_copies(block):
            copy.start()
    z_copy("near", 0).wait_recv()

    @pl.when(is_outer)
    def _():
        z_copy("end_a", 1).start()
        z_copy("near", 1).start()

    @pl.when(is_inner)
    def _():
        z_copy("mid_near", 0).start()
        z_copy("mid_own", 0).wait_recv()
        z_copy("end_inner", 0).start()
        for piece in both:
            z_copy("mid_own", 1, piece).start()

    plane[0].second()

    @pl.when(is_outer)
    def _():
        z_copy("end_a", 1).wait_send()
        z_copy("end_a", 2).start()
        z_copy("near", 2).start()
        plane[1].first()

    @pl.when(is_inner)
    def _():
        z_copy("end_a", 1).wait_recv()
        ends[0].first()
        z_copy("mid_near", 0).wait_recv()
        z_copy("end_outer", 0).start()
        z_copy("near", 1).wait_recv()
        for piece in both:
            z_copy("mid_near", 1, piece).start()
        for piece in both:
            z_copy("mid_own", 2, piece).start()
        ends[0].second()
        plane[1].first()

    plane[0].third()

    @pl.when(is_inner)
    def _():
        ends[0].third()
        z_copy("end_a", 2).wait_recv()
        ends[1].first()
        ends[0].finish()
        help_end(1, 0)
        help_end(1, 1)
        z_copy("near", 2).wait_recv()
        for piece in both:
            z_copy("mid_near", 2, piece).start()
        ends[1].second()

    plane[1].second()
    plane[2].first()

    @pl.when(is_inner)
    def _():
        ends[1].third()

    plane[1].third()
    multiply(0)

    @pl.when(is_inner)
    def _():
        ends[1].finish()
        help_end(2, 0)
        help_end(2, 1)

    plane[2].second()
    plane[2].third()
    multiply(1)
    multiply(2)

    for gather in plane:
        gather.drain()
    z_copy("near", 0).wait_send()

    @pl.when(is_outer)
    def _():
        z_copy("near", 1).wait_send()
        z_copy("near", 2).wait_send()
        z_copy("end_a", 2).wait_send()

    @pl.when(is_inner)
    def _():
        for gather in ends:
            gather.drain()
        for kind in ("mid_own", "mid_near", "end_inner", "end_outer"):
            z_copy(kind, 0).wait_send()
        for block in HELPED:
            for piece in both:
                for kind in ("mid_own", "mid_near", "part"):
                    z_copy(kind, block, piece).wait_send()


def linked_body(
    amplitudes,
    integrals,
    occupied_irrep,
    virtual_order,
    block_irreps,
    occupied_energy,
    virtual_energy,
):
    blocks, virt_local, occ_local, pair_width = amplitudes.shape
    depth, column_width = integrals.shape[1:]
    rows = virt_local * occ_local
    shift = shift_table(
        occupied_irrep, virtual_order, block_irreps, occupied_energy, virtual_energy
    )
    row_shift = lax.dynamic_slice_in_dim(shift, lax.axis_index("row") * occ_local, occ_local, 2)
    col_shift = lax.dynamic_slice_in_dim(
        shift.reshape(blocks, pair_width), lax.axis_index("pair") * column_width, column_width, 1
    )
    cycle_term = pl.pallas_call(
        kernel,
        out_shape=(
            jax.ShapeDtypeStruct((blocks, 8 * rows, column_width), jnp.float32),
            jax.ShapeDtypeStruct((blocks, 8, rows, pair_width), jnp.bfloat16),
            jax.ShapeDtypeStruct((blocks, 4, depth, column_width), jnp.bfloat16),
            jax.ShapeDtypeStruct((2, 8, rows, pair_width - depth), jnp.bfloat16),
            jax.ShapeDtypeStruct((2, 8 * rows, column_width), jnp.float32),
            jax.ShapeDtypeStruct((2, 8 * rows, column_width), jnp.float32),
        ),
        in_specs=[pl.BlockSpec(memory_space=pl.ANY)] * 2,
        out_specs=(pl.BlockSpec(memory_space=pl.ANY),) * 6,
        scratch_shapes=[
            pltpu.SemaphoreType.DMA((14, blocks)),
            pltpu.SemaphoreType.DMA((14, blocks)),
            pltpu.SemaphoreType.DMA((8, blocks + 2)),
            pltpu.SemaphoreType.DMA((8, blocks + 2)),
            pltpu.SemaphoreType.DMA((2, blocks)),
        ],
        compiler_params=pltpu.CompilerParams(
            collective_id=0, has_side_effects=True, vmem_limit_bytes=50 * 2**20
        ),
    )(amplitudes.reshape(blocks, rows, pair_width), integrals)[0]
    cycle_term = cycle_term.reshape(blocks, 8 * virt_local, occ_local, column_width)
    return cycle_term / (row_shift[..., None] + col_shift[:, None, None, :])


def solution(mesh):
    placed = (P(None, "pair", "row", None), P(None, "row", "pair"), P(), P(), P(), P(), P())
    linked = mesh.shape["pair"] == 8 and mesh.shape["row"] == 4
    return jax.shard_map(
        linked_body if linked else body,
        mesh=mesh,
        in_specs=placed,
        out_specs=P(None, None, "row", "pair"),
        check_vma=False,
    )
```

```python
import jax
import jax.numpy as jnp
from jax import lax
from jax.experimental import pallas as pl
from jax.experimental.pallas import tpu as pltpu
from jax.sharding import PartitionSpec as P

VIRG = 160


def shift_table(occupied_irrep, virtual_order, block_irreps, occupied_energy, virtual_energy):
    count_virt = virtual_energy.shape[0]
    orbital_ids = jnp.arange(count_virt, dtype=jnp.int32)
    matches = virtual_order[:, None] == orbital_ids[None, :]
    slot_energy = jnp.sum(jnp.where(matches, virtual_energy[None, :], jnp.float32(0.0)), axis=1)
    irrep_count = count_virt // VIRG
    energy_grid = slot_energy.reshape(irrep_count, VIRG)
    pair_irrep = jnp.bitwise_xor(block_irreps[:, None], occupied_irrep[None, :])
    irrep_ids = jnp.arange(irrep_count, dtype=jnp.int32)
    chosen = pair_irrep[:, None, None, :] == irrep_ids[None, :, None, None]
    picked = jnp.sum(jnp.where(chosen, energy_grid[None, :, :, None], jnp.float32(0.0)), axis=1)
    return picked - occupied_energy[None, None, :]


def body(
    amplitudes,
    integrals,
    occupied_irrep,
    virtual_order,
    block_irreps,
    occupied_energy,
    virtual_energy,
):
    block_count, virt_local, occ_local, pair_width = amplitudes.shape
    column_width = integrals.shape[2]
    shift = shift_table(
        occupied_irrep, virtual_order, block_irreps, occupied_energy, virtual_energy
    )
    occ_start = lax.axis_index("row") * occ_local
    col_start = lax.axis_index("pair") * column_width
    results = []
    for block in range(block_count):
        whole_rows = lax.all_gather(integrals[block], "row", axis=0, tiled=True)
        piece = lax.all_gather(amplitudes[block], "pair", axis=0, tiled=True)
        flat = piece.reshape(piece.shape[0] * piece.shape[1], piece.shape[2])
        product = jnp.dot(flat, whole_rows, preferred_element_type=jnp.float32)
        cycle_term = product.reshape(piece.shape[0], piece.shape[1], whole_rows.shape[1])
        row_shift = lax.dynamic_slice_in_dim(shift[block], occ_start, occ_local, 1)
        col_shift = lax.dynamic_slice_in_dim(
            shift[block].reshape(pair_width), col_start, column_width, 0
        )
        denominator = row_shift[:, :, None] + col_shift[None, None, :]
        results.append(cycle_term / denominator)
    return jnp.stack(results)


def kernel(a_ref, b_ref, cycle_ref, all_a, all_b, partial, z_send, z_recv, p_send, p_recv, own_sem):
    blocks = a_ref.shape[0]
    pair = lax.axis_index("pair")
    row = lax.axis_index("row")
    near = row ^ 1
    across = 3 - row
    is_inner = (row == 1) | (row == 2)

    barrier = pltpu.get_barrier_semaphore()
    friends = [(pair, near), (pair, across)] + [(pair ^ step, row) for step in (1, 2, 4, 6)]
    for friend in friends:
        pl.semaphore_signal(
            barrier, inc=1, device_id=friend, device_id_type=pl.DeviceIdType.MESH
        )
    pl.semaphore_wait(barrier, len(friends))

    def z_copy(kind, block):
        source, slot, target = {
            "near": (b_ref.at[block], row, near),
            "mid_own": (b_ref.at[block], row, across),
            "mid_near": (all_b.at[block, near], near, across),
            "end_inner": (all_b.at[block, across], across, near),
            "end_outer": (all_b.at[block, across ^ 1], across ^ 1, near),
        }[kind]
        place = ["near", "mid_own", "mid_near", "end_inner", "end_outer"].index(kind)
        return pltpu.make_async_remote_copy(
            src_ref=source,
            dst_ref=all_b.at[block, slot],
            send_sem=z_send.at[place, block],
            recv_sem=z_recv.at[place, block],
            device_id=(pair, target),
            device_id_type=pl.DeviceIdType.MESH,
        )

    def plane_copy(step, block):
        return pltpu.make_async_remote_copy(
            src_ref=a_ref.at[block],
            dst_ref=all_a.at[block, pair],
            send_sem=p_send.at[step - 1, block],
            recv_sem=p_recv.at[step - 1, block],
            device_id=(pair ^ (2 * step), row),
            device_id_type=pl.DeviceIdType.MESH,
        )

    def core_copy(step, block):
        piece = pair ^ (2 * step)
        return pltpu.make_async_remote_copy(
            src_ref=a_ref.at[block] if step == 0 else all_a.at[block, piece],
            dst_ref=all_a.at[block, piece],
            send_sem=p_send.at[3 + step, block],
            recv_sem=p_recv.at[3 + step, block],
            device_id=(pair ^ 1, row),
            device_id_type=pl.DeviceIdType.MESH,
        )

    def own_copies(block):
        return [
            pltpu.make_async_copy(a_ref.at[block], all_a.at[block, pair], own_sem.at[0, block]),
            pltpu.make_async_copy(b_ref.at[block], all_b.at[block, row], own_sem.at[1, block]),
        ]

    def plane_start(block):
        for step in (1, 2, 3):
            plane_copy(step, block).start()
        core_copy(0, block).start()

    def plane_forward(block):
        for step in (1, 2, 3):
            plane_copy(step, block).wait_recv()
            core_copy(step, block).start()

    def arrived(block):
        for copy in own_copies(block):
            copy.wait()
        for step in range(4):
            core_copy(step, block).wait_recv()

        @pl.when(jnp.logical_not(is_inner))
        def _():
            z_copy("end_inner", block).wait_recv()

    def last_arrived(block):
        @pl.when(jnp.logical_not(is_inner))
        def _():
            z_copy("end_outer", block).wait_recv()

    def multiply(block, first, parts, goal, extra=()):
        count, rows, _ = all_a.shape[1:]
        depth, columns = all_b.shape[2:]

        def tile(a_tile, b_tile, *rest):
            def add(part, total):
                start = pl.multiple_of(part * depth, depth)
                left = a_tile[:, :, pl.ds(start, depth)].reshape(2 * rows, depth)
                return total + jnp.dot(left, b_tile[part], preferred_element_type=jnp.float32)

            begin = rest[0][...] if extra else jnp.zeros(rest[-1].shape, jnp.float32)
            rest[-1][...] = lax.fori_loop(0, parts, add, begin)

        square = pl.BlockSpec((2 * rows, columns), lambda i: (i, 0))
        start = pl.multiple_of(first * depth, depth)
        pltpu.emit_pipeline(
            tile,
            grid=(count // 2,),
            in_specs=[
                pl.BlockSpec((2, rows, parts * depth), lambda i: (i, 0, 0)),
                pl.BlockSpec((parts, depth, columns), lambda i: (0, 0, 0)),
            ]
            + [square] * len(extra),
            out_specs=[square],
        )(
            all_a.at[block, :, :, pl.ds(start, parts * depth)],
            all_b.at[block, pl.ds(first, parts)],
            *extra,
            goal,
        )

    z_copy("near", 0).start()
    plane_start(0)

    @pl.when(is_inner)
    def _():
        z_copy("mid_own", 0).start()

    plane_start(1)
    for block in range(blocks):
        for copy in own_copies(block):
            copy.start()
    for block in range(blocks):
        z_copy("near", block).wait_recv()
        if block + 1 < blocks:
            z_copy("near", block + 1).start()

        @pl.when(is_inner)
        def _():
            z_copy("mid_near", block).start()
            z_copy("mid_own", block).wait_recv()
            z_copy("end_inner", block).start()
            if block + 1 < blocks:
                z_copy("mid_own", block + 1).start()
            z_copy("mid_near", block).wait_recv()
            z_copy("end_outer", block).start()

        plane_forward(block)
        if block + 2 < blocks:
            plane_start(block + 2)
        if block >= 1 and block + 1 < blocks:
            arrived(block - 1)
            last_arrived(block - 1)
            multiply(block - 1, 0, 4, cycle_ref.at[block - 1])
    arrived(blocks - 2)
    last_arrived(blocks - 2)
    multiply(blocks - 2, 0, 4, cycle_ref.at[blocks - 2])
    arrived(blocks - 1)
    multiply(blocks - 1, row // 2, 3, partial)
    last_arrived(blocks - 1)
    multiply(blocks - 1, 3 * (1 - row // 2), 1, cycle_ref.at[blocks - 1], (partial,))
    for block in range(blocks):
        z_copy("near", block).wait_send()
        for step in (1, 2, 3):
            plane_copy(step, block).wait_send()
        for step in range(4):
            core_copy(step, block).wait_send()

        @pl.when(is_inner)
        def _():
            for kind in ("mid_own", "mid_near", "end_inner", "end_outer"):
                z_copy(kind, block).wait_send()


def linked_body(
    amplitudes,
    integrals,
    occupied_irrep,
    virtual_order,
    block_irreps,
    occupied_energy,
    virtual_energy,
):
    blocks, virt_local, occ_local, pair_width = amplitudes.shape
    depth, column_width = integrals.shape[1:]
    rows = virt_local * occ_local
    shift = shift_table(
        occupied_irrep, virtual_order, block_irreps, occupied_energy, virtual_energy
    )
    row_shift = lax.dynamic_slice_in_dim(shift, lax.axis_index("row") * occ_local, occ_local, 2)
    col_shift = lax.dynamic_slice_in_dim(
        shift.reshape(blocks, pair_width), lax.axis_index("pair") * column_width, column_width, 1
    )
    cycle_term = pl.pallas_call(
        kernel,
        out_shape=(
            jax.ShapeDtypeStruct((blocks, 8 * rows, column_width), jnp.float32),
            jax.ShapeDtypeStruct((blocks, 8, rows, pair_width), jnp.bfloat16),
            jax.ShapeDtypeStruct((blocks, 4, depth, column_width), jnp.bfloat16),
            jax.ShapeDtypeStruct((8 * rows, column_width), jnp.float32),
        ),
        in_specs=[pl.BlockSpec(memory_space=pl.ANY)] * 2,
        out_specs=(pl.BlockSpec(memory_space=pl.ANY),) * 4,
        scratch_shapes=[
            pltpu.SemaphoreType.DMA((5, blocks)),
            pltpu.SemaphoreType.DMA((5, blocks)),
            pltpu.SemaphoreType.DMA((7, blocks)),
            pltpu.SemaphoreType.DMA((7, blocks)),
            pltpu.SemaphoreType.DMA((2, blocks)),
        ],
        compiler_params=pltpu.CompilerParams(
            collective_id=0, has_side_effects=True, vmem_limit_bytes=50 * 2**20
        ),
    )(amplitudes.reshape(blocks, rows, pair_width), integrals)[0]
    cycle_term = cycle_term.reshape(blocks, 8 * virt_local, occ_local, column_width)
    return cycle_term / (row_shift[..., None] + col_shift[:, None, None, :])


def solution(mesh):
    placed = (P(None, "pair", "row", None), P(None, "row", "pair"), P(), P(), P(), P(), P())
    linked = mesh.shape["pair"] == 8 and mesh.shape["row"] == 4
    return jax.shard_map(
        linked_body if linked else body,
        mesh=mesh,
        in_specs=placed,
        out_specs=P(None, None, "row", "pair"),
        check_vma=False,
    )
```
